1024 devices in a mesh: replica: 16 (over x, z_hi), fsdp: 64 (over y, z_lo, core).
Axes of the slice: x: 4, y: 8, z: 16 (z_hi: 4, z_lo: 4; z = z_hi * 4 + z_lo), core: 2. Of those that a mesh axis runs over, the one named last changes fastest.
Arguments:
- queries: bfloat16 [16, 8192, 2048], P('replica', 'fsdp'), may hold values from -6 to 6, as said below
- key_rows: bfloat16 [16, 8192, 2048], P('replica', 'fsdp'), may hold values from -6 to 6
- value_rows: bfloat16 [16, 8192, 2048], P('replica', 'fsdp'), may hold values from -6 to 6
- cotangent: bfloat16 [16, 20, 8192], P('replica', None, 'fsdp'), may hold values from -6 to 6
- readout: float32 [16, 20, 2048], P('replica', None, 'fsdp'), may hold values from -3 to 3
- rand_blocks: int32 [64, 2], replicated, may hold values from 0 to 63
- global_blocks: int32 [1], replicated, may hold values from 0 to 63
- hyper_dim: int32 [20], replicated, may hold values from 0 to 3
Outputs:
- attention: bfloat16 [16, 8192, 2048], P('replica', 'fsdp')
- new_readout: float32 [16, 20, 2048], P('replica', None, 'fsdp')
The draws below stay inside these ranges and needn't reach their ends.
Inputs may be any that keep to these rules, and one draw needn't show every extreme that they name: `queries`: queries and keys lie within the range. `rand_blocks`: each entry names a block of the window; it may repeat a window or global block.
All inputs are finite; a program needn't handle non-finite values.
Results may differ from the reference program's by a relative error of at most 0.0049.
Values may be sent and summed in bfloat16 or wider, within the bound.
No kernel may reach another device: no remote copies, remote signals or barrier semaphores. Data moves between devices by JAX's collectives and lax.ppermute only.
A program may use at most 64 MiB of HBM per device.

```python
import jax
import jax.numpy as jnp
from jax import lax

BLOCK = 128
HEADS = 16
HEAD_SIZE = 128
JOINTS = 20
RANDOM = 2
GLOBALS = 1
HD = 2048
REPS = 16
TOKENS = 8192
NB = 64
HYPER_BITS = 4


def drawn_pair(key):
    base_key = jax.random.fold_in(key, 7)
    key_one, key_two = jax.random.split(base_key, 2)
    width = HEADS * HEAD_SIZE
    shape = (REPS, TOKENS, width)
    query_part = jnp.clip(jax.random.normal(key_one, shape, jnp.float32), -4.5, 4.5)
    key_part = jnp.clip(jax.random.normal(key_two, shape, jnp.float32), -4.5, 4.5)
    return (query_part, key_part)


def draw_queries(key, part):
    return drawn_pair(key)[0].astype(jnp.bfloat16)


def draw_key_rows(key, part):
    return drawn_pair(key)[1].astype(jnp.bfloat16)


def plant(drawn, rng, least, top_value):
    index_at = [jax.random.randint(jax.random.fold_in(rng, axis), (), 0, length) for axis, length in enumerate(drawn.shape)]
    main_axis = drawn.shape.index(max(drawn.shape))
    next_to = index_at[:main_axis] + [(index_at[main_axis] + 1) % drawn.shape[main_axis]] + index_at[main_axis + 1:]
    return drawn.at[tuple(index_at)].set(least).at[tuple(next_to)].set(top_value)


def levels(own_key, extent, shards, least, largest):
    def one(position, blocks):
        draws = jax.random.uniform(jax.random.fold_in(jax.random.fold_in(own_key, 6), position), (blocks,), jnp.float32, least / len(shards), largest / len(shards))
        return jnp.repeat(jnp.exp(draws), extent[position] // blocks).reshape((-1,) + (1,) * (len(extent) - position - 1))

    gain = one(*shards[0])
    for cut in shards[1:]:
        gain = gain * one(*cut)
    return gain


def gaussian(stream_key, dims, scale, reach, shards=(), held_as=jnp.bfloat16):
    factor_of = levels(stream_key, dims, shards, -0.22, 0.18) if shards else 1.0
    values = jax.random.normal(stream_key, dims, jnp.float32) * scale * factor_of
    return jnp.minimum(jnp.maximum(values, -reach), reach).astype(held_as)


def setup_inputs(seed: int = 0) -> dict:
    key_list = jax.random.split(jax.random.key(seed), 9)
    return {
        "queries": draw_queries(jax.random.fold_in(key_list[8], 71), 0),
        "key_rows": draw_key_rows(jax.random.fold_in(key_list[8], 71), 0),
        "value_rows": gaussian(key_list[2], (REPS, TOKENS, HD), 1.0, 6.0, ((0, 16), (1, 64))),
        "cotangent": gaussian(key_list[3], (REPS, JOINTS, TOKENS), 1.0, 6.0, ((0, 16), (2, 64))),
        "readout": gaussian(key_list[4], (REPS, JOINTS, HD), 0.5, 3.0, ((0, 16), (2, 64)), jnp.float32),
        "rand_blocks": plant(jax.random.randint(key_list[5], (NB, RANDOM), 0, NB), jax.random.fold_in(key_list[5], 1), 0, NB - 1).astype(jnp.int32),
        "global_blocks": jax.random.randint(key_list[6], (GLOBALS,), 0, NB).astype(jnp.int32),
        "hyper_dim": plant(jax.random.randint(key_list[7], (JOINTS,), 0, HYPER_BITS), jax.random.fold_in(key_list[7], 1), 0, HYPER_BITS - 1).astype(jnp.int32),
    }


def key_table(rand_blocks, global_blocks):
    block_ids = jnp.arange(NB, dtype=jnp.int32)
    columns = jnp.concatenate([block_ids[:, None], (block_ids - 1)[:, None], (block_ids + 1)[:, None], rand_blocks.astype(jnp.int32), jnp.broadcast_to(global_blocks.astype(jnp.int32)[None, :], (NB, GLOBALS))], axis=1)
    usable = (columns >= 0) & (columns < NB)
    return jnp.clip(columns, 0, NB - 1), usable


def replica_attention(query_rows, key_rows, value_rows, table, usable):
    key_blocks = key_rows.reshape(NB, BLOCK, HEADS, HEAD_SIZE)
    value_blocks = value_rows.reshape(NB, BLOCK, HEADS, HEAD_SIZE)
    query_blocks = query_rows.reshape(NB, BLOCK, HEADS, HEAD_SIZE)

    def one_block(block):
        chosen = table[block]
        key_set = key_blocks[chosen].reshape(-1, HEADS, HEAD_SIZE).astype(jnp.float32)
        value_set = value_blocks[chosen].reshape(-1, HEADS, HEAD_SIZE).astype(jnp.float32)
        query_set = query_blocks[block].astype(jnp.float32)
        scores = jnp.einsum("qhd,khd->hqk", query_set, key_set) * (HEAD_SIZE ** -0.5)
        key_mask = jnp.repeat(usable[block], BLOCK)
        scores = jnp.where(key_mask[None, None, :], scores, -jnp.inf)
        chances = jax.nn.softmax(scores, axis=-1).astype(jnp.bfloat16)
        mixed = jnp.einsum("hqk,khd->qhd", chances.astype(jnp.float32), value_set)
        return mixed.reshape(BLOCK, HEADS * HEAD_SIZE).astype(jnp.bfloat16)

    return lax.map(one_block, jnp.arange(NB, dtype=jnp.int32)).reshape(TOKENS, HEADS * HEAD_SIZE)


def reference(queries, key_rows, value_rows, cotangent, readout, rand_blocks, global_blocks, hyper_dim):
    table, usable = key_table(rand_blocks, global_blocks)

    def per_replica(inputs):
        query_rows, keys_here, values_here, grad_out = inputs
        output = replica_attention(query_rows, keys_here, values_here, table, usable)
        gradient = jnp.dot(grad_out, output, preferred_element_type=jnp.float32)
        return output, gradient

    attention, gradients = lax.map(per_replica, (queries, key_rows, value_rows, cotangent))
    stepped = readout - 0.01 * gradients
    replica_ids = jnp.arange(REPS, dtype=jnp.int32)
    masks = jnp.left_shift(jnp.int32(1), hyper_dim.astype(jnp.int32))
    partner_ids = jnp.bitwise_xor(replica_ids[:, None], masks[None, :])
    joint_ids = jnp.arange(JOINTS, dtype=jnp.int32)
    partner_rows = stepped[partner_ids, joint_ids[None, :]]
    new_readout = 0.5 * (stepped + partner_rows)
    return attention, new_readout
```

```python
import functools

import jax
import jax.numpy as jnp
from jax import lax
from jax.experimental import pallas as pl
from jax.experimental.pallas import tpu as pltpu
from jax.sharding import Mesh, PartitionSpec as P

BLOCK = 128
HEAD_SIZE = 128
LEARN_RATE = 0.01
MEMBERS = 4
MEMBER_BITS = 2
LANES = 128
UNROLL = 4
SUBLANES = 8
LOG2_E = 1.4426950408889634


def split_heads(rows_ref, out_ref):
    for head in range(out_ref.shape[0]):
        out_ref[head] = rows_ref[:, head * HEAD_SIZE : (head + 1) * HEAD_SIZE]


def split_queries(query_ref, cot_ref, out_ref):
    heads, rows, _ = out_ref.shape
    joints = cot_ref.shape[0]
    tail = jnp.concatenate(
        [cot_ref[...], jnp.zeros((rows - BLOCK - joints, BLOCK), cot_ref.dtype)], axis=0
    )
    for head in range(heads):
        out_ref[head, :BLOCK, :] = query_ref[:, head * HEAD_SIZE : (head + 1) * HEAD_SIZE]
        out_ref[head, BLOCK:, :] = tail


def join_heads(parts_ref, out_ref):
    for head in range(parts_ref.shape[0]):
        out_ref[:, head * HEAD_SIZE : (head + 1) * HEAD_SIZE] = parts_ref[head]


def attend(
    joints,
    rand_ref,
    global_ref,
    query_ref,
    k0, k1, k2, k3,
    v0, v1, v2, v3,
    readout_ref,
    out_ref,
    own_ref,
    near_ref,
    far_ref,
    cross_ref,
    key_all,
    value_all,
    grad_ref,
    hold_ref,
    sems,
):
    member = lax.axis_index("member")
    per_member = query_ref.shape[0]
    blocks = per_member * MEMBERS
    shard = readout_ref.shape[2]
    per_row = LANES // shard
    part_rows = joints // per_row
    copies = []
    for at, source in enumerate((k0, k1, k2, k3)):
        copies.append(pltpu.make_async_copy(source, key_all.at[at], sems.at[at]))
    for at, source in enumerate((v0, v1, v2, v3)):
        copies.append(pltpu.make_async_copy(source, value_all.at[at], sems.at[MEMBERS + at]))
    for copy in copies:
        copy.start()
    hold_ref[...] = jnp.zeros_like(hold_ref)
    for joint in range(joints):
        hold_ref[joint : joint + 1, :shard] = readout_ref[joint]
    grad_ref[...] = jnp.zeros_like(grad_ref)
    for copy in copies:
        copy.wait()
    factor = (HEAD_SIZE ** (-0.5)) * LOG2_E

    def one_block(at, carry):
        block = at * MEMBERS + member
        listed = [block, jnp.maximum(block - 1, 0), jnp.minimum(block + 1, blocks - 1)]
        listed += [rand_ref[c, block] for c in range(rand_ref.shape[0])]
        listed += [global_ref[c] for c in range(global_ref.shape[0])]
        places = [((b & (MEMBERS - 1)) ^ member, b >> MEMBER_BITS) for b in listed]
        keys = jnp.concatenate([key_all[p, s] for p, s in places], axis=0)
        values = jnp.concatenate([value_all[p, s] for p, s in places], axis=0)
        scores = lax.dot_general(
            query_ref[at, :BLOCK, :],
            keys,
            (((1,), (1,)), ((), ())),
            preferred_element_type=jnp.float32,
        )
        before = jnp.where(block >= 1, 0.0, -jnp.inf).astype(jnp.float32)
        after = jnp.where(block + 1 < blocks, 0.0, -jnp.inf).astype(jnp.float32)
        scores = jnp.concatenate(
            [
                scores[:, :BLOCK],
                scores[:, BLOCK : 2 * BLOCK] + before,
                scores[:, 2 * BLOCK : 3 * BLOCK] + after,
                scores[:, 3 * BLOCK :],
            ],
            axis=1,
        )
        row_max = jnp.max(scores, axis=1, keepdims=True)
        weights = jnp.exp2((scores - row_max) * factor)
        total = jnp.sum(weights, axis=1, keepdims=True)
        chances = (weights * (1.0 / total)).astype(jnp.bfloat16)
        mixed = jnp.dot(chances, values, preferred_element_type=jnp.float32)
        mixed = mixed.astype(jnp.bfloat16)
        out_ref[at] = mixed
        grad_ref[...] += jnp.dot(
            query_ref[at, BLOCK:, :], mixed, preferred_element_type=jnp.float32
        )
        return carry

    lax.fori_loop(0, per_member, one_block, 0, unroll=UNROLL)

    lane = lax.broadcasted_iota(jnp.int32, (SUBLANES, LANES), 1) // shard

    def packed(source_ref, first):
        piece = jnp.zeros((SUBLANES, LANES), jnp.float32)
        for j in range(per_row):
            rows = source_ref[j * part_rows : j * part_rows + SUBLANES, :]
            turn = (j * shard - first) % LANES
            rows = pltpu.roll(rows, turn, 1) if turn else rows
            piece = jnp.where(lane == j, rows, piece)
        return piece

    pieces = [-LEARN_RATE * packed(grad_ref, other * shard) for other in range(MEMBERS)]

    def piece_of(wanted):
        piece = pieces[0]
        for other in range(1, MEMBERS):
            piece = jnp.where(wanted == other, pieces[other], piece)
        return piece

    own_ref[...] = packed(hold_ref, 0) + piece_of(member)
    near_ref[...] = piece_of(member ^ 1)
    far_ref[...] = piece_of(member ^ 2)
    cross_ref[...] = piece_of(member ^ 3)


def blend(joints, hyper_ref, own_ref, *refs):
    partner_refs, out_ref = refs[:-1], refs[-1]
    shard = out_ref.shape[2]
    per_row = LANES // shard
    part_rows = joints // per_row
    lane = lax.broadcasted_iota(jnp.int32, (SUBLANES, LANES), 1) // shard
    row = lax.broadcasted_iota(jnp.int32, (SUBLANES, LANES), 0)
    joint = jnp.where(row < part_rows, lane * part_rows + row, joints)
    dims = jnp.zeros((SUBLANES, LANES), jnp.int32)
    for j in range(joints):
        dims = jnp.where(joint == j, hyper_ref[j], dims)
    own = own_ref[...]
    partner = own
    for bit, ref in enumerate(partner_refs):
        partner = jnp.where(dims == bit, ref[...], partner)
    mixed = 0.5 * (own + partner)
    for j in range(per_row):
        turn = (-j * shard) % LANES
        part = pltpu.roll(mixed, turn, 1) if turn else mixed
        for r in range(part_rows):
            out_ref[j * part_rows + r] = part[r : r + 1, :shard]


def local(queries, key_rows, value_rows, cotangent, readout, rand_blocks, global_blocks, hyper_dim):
    heads = lax.axis_size("head")
    replicas = lax.axis_size("replica")
    joints = cotangent.shape[1]
    shard = readout.shape[2]
    cot_rows = -(-joints // 32) * 32
    vmem = pl.BlockSpec(memory_space=pltpu.VMEM)
    smem = pl.BlockSpec(memory_space=pltpu.SMEM)
    anywhere = pl.BlockSpec(memory_space=pl.ANY)
    by_head = (heads, BLOCK, HEAD_SIZE)

    def spread(value):
        return lax.all_to_all(value, "head", split_axis=0, concat_axis=0, tiled=True)

    def swap(value, distance):
        return lax.ppermute(value, "member", [(i, i ^ distance) for i in range(MEMBERS)])

    def split(rows):
        return pl.pallas_call(
            split_heads,
            out_shape=jax.ShapeDtypeStruct(by_head, rows.dtype),
            in_specs=[vmem],
            out_specs=vmem,
        )(rows)

    split_k = split(key_rows[0])
    k0 = spread(split_k)
    split_v = split(value_rows[0])
    v0 = spread(split_v)
    packed = pl.pallas_call(
        split_queries,
        out_shape=jax.ShapeDtypeStruct((heads, BLOCK + cot_rows, HEAD_SIZE), queries.dtype),
        in_specs=[vmem, vmem],
        out_specs=vmem,
        name="split_queries",
    )(queries[0], cotangent[0])
    q0 = spread(packed)
    k2 = swap(k0, 2)
    k1 = swap(k0, 1)
    k3 = swap(k2, 1)
    v2 = swap(v0, 2)
    v1 = swap(v0, 1)
    v3 = swap(v2, 1)
    piece = jax.ShapeDtypeStruct((SUBLANES, LANES), jnp.float32)
    mixed, own, near, far, cross = pl.pallas_call(
        functools.partial(attend, joints),
        out_shape=(jax.ShapeDtypeStruct(by_head, jnp.bfloat16), piece, piece, piece, piece),
        in_specs=[smem, smem, vmem] + [anywhere] * 8 + [vmem],
        out_specs=(vmem,) * 5,
        scratch_shapes=[
            pltpu.VMEM((MEMBERS, *by_head), jnp.bfloat16),
            pltpu.VMEM((MEMBERS, *by_head), jnp.bfloat16),
            pltpu.VMEM((cot_rows, HEAD_SIZE), jnp.float32),
            pltpu.VMEM((cot_rows, LANES), jnp.float32),
            pltpu.SemaphoreType.DMA((2 * MEMBERS,)),
        ],
        name="attend",
    )(
        rand_blocks.T,
        global_blocks,
        q0,
        k0, k1, k2, k3,
        v0, v1, v2, v3,
        readout.reshape(joints, 1, shard),
    )
    near = swap(near, 1)
    far = swap(far, 2)
    cross = swap(cross, 3)
    returned = spread(mixed)
    stepped = (own + near) + (far + cross)
    partners = []
    for bit in range(replicas.bit_length() - 1):
        partners.append(
            lax.ppermute(
                stepped, "replica", [(i, i ^ 1 << bit) for i in range(replicas)]
            )
        )
    new_readout = pl.pallas_call(
        functools.partial(blend, joints),
        out_shape=jax.ShapeDtypeStruct((joints, 1, shard), jnp.float32),
        in_specs=[smem] + [vmem] * (1 + len(partners)),
        out_specs=vmem,
        name="blend",
    )(hyper_dim, stepped, *partners)
    attention = pl.pallas_call(
        join_heads,
        out_shape=jax.ShapeDtypeStruct((BLOCK, heads * HEAD_SIZE), returned.dtype),
        in_specs=[vmem],
        out_specs=vmem,
        name="join_heads",
    )(returned)
    return (attention[None], new_readout.reshape(1, joints, shard))


def solution(mesh):
    replicas, group = mesh.devices.shape
    fine = Mesh(
        mesh.devices.reshape(replicas, group // MEMBERS, MEMBERS),
        ("replica", "head", "member"),
    )
    rows = P("replica", ("head", "member"), None)
    columns = P("replica", None, ("head", "member"))
    return jax.shard_map(
        local,
        mesh=fine,
        in_specs=(rows, rows, rows, columns, columns, P(), P(), P()),
        out_specs=(rows, columns),
        check_vma=False,
    )
```

```python
import functools

import jax
import jax.numpy as jnp
from jax import lax
from jax.experimental import pallas as pl
from jax.experimental.pallas import tpu as pltpu
from jax.sharding import Mesh, PartitionSpec as P

BLOCK = 128
HEAD_SIZE = 128
LEARN_RATE = 0.01
MEMBERS = 4
MEMBER_BITS = 2
LANES = 128
VMEM_LIMIT = 20 << 20
UNROLL = True
ROW_TILE = 32
SUBLANES = 8
LOG2_E = 1.4426950408889634


def split_heads(rows_ref, out_ref):
    for head in range(out_ref.shape[0]):
        out_ref[head] = rows_ref[:, head * HEAD_SIZE : (head + 1) * HEAD_SIZE]


def split_queries(query_ref, cot_ref, out_ref):
    heads, rows, _ = out_ref.shape
    joints = cot_ref.shape[0]
    tail = jnp.concatenate(
        [cot_ref[...], jnp.zeros((rows - BLOCK - joints, BLOCK), cot_ref.dtype)], axis=0
    )
    for head in range(heads):
        out_ref[head, :BLOCK, :] = query_ref[:, head * HEAD_SIZE : (head + 1) * HEAD_SIZE]
        out_ref[head, BLOCK:, :] = tail


def join_heads(parts_ref, out_ref):
    for head in range(parts_ref.shape[0]):
        out_ref[:, head * HEAD_SIZE : (head + 1) * HEAD_SIZE] = parts_ref[head]


def attend(
    joints,
    rand_ref,
    global_ref,
    query_ref,
    k0, k1, k2, k3,
    v0, v1, v2, v3,
    readout_ref,
    out_ref,
    sent_ref,
    key_all,
    value_all,
    grad_ref,
    hold_ref,
    s_even,
    s_odd,
    p_even,
    p_odd,
    sems,
):
    member = lax.axis_index("member")
    per_member = query_ref.shape[0]
    blocks = per_member * MEMBERS
    shard = readout_ref.shape[2]
    per_row = LANES // shard
    part_rows = joints // per_row
    early = ((k0, key_all.at[0]), (k1, key_all.at[1]), (k2, key_all.at[2]), (v0, value_all.at[0]))
    copies = [pltpu.make_async_copy(*pair, sems.at[at]) for at, pair in enumerate(early)]
    for copy in copies:
        copy.start()
    key_all[3] = k3[...]
    for at, source in ((1, v1), (2, v2), (3, v3)):
        value_all[at] = source[...]
    hold_ref[...] = jnp.zeros_like(hold_ref)
    for joint in range(joints):
        hold_ref[joint : joint + 1, :shard] = readout_ref[joint]
    for copy in copies:
        copy.wait()
    factor = (HEAD_SIZE ** (-0.5)) * LOG2_E

    def listed(at):
        block = at * MEMBERS + member
        ids = [block, jnp.maximum(block - 1, 0), jnp.minimum(block + 1, blocks - 1)]
        ids += [rand_ref[c, block] for c in range(rand_ref.shape[0])]
        ids += [global_ref[c] for c in range(global_ref.shape[0])]
        return block, [((b & (MEMBERS - 1)) ^ member, b >> MEMBER_BITS) for b in ids]

    def score(at, into):
        block, places = listed(at)
        keys = jnp.concatenate([key_all[p, s] for p, s in places], axis=0)
        scores = lax.dot_general(
            query_ref[at, :BLOCK, :],
            keys,
            (((1,), (1,)), ((), ())),
            preferred_element_type=jnp.float32,
        )
        before = jnp.where(block >= 1, 0.0, -jnp.inf).astype(jnp.float32)
        after = jnp.where(block + 1 < blocks, 0.0, -jnp.inf).astype(jnp.float32)
        into[:, :BLOCK] = scores[:, :BLOCK]
        into[:, BLOCK : 2 * BLOCK] = scores[:, BLOCK : 2 * BLOCK] + before
        into[:, 2 * BLOCK : 3 * BLOCK] = scores[:, 2 * BLOCK : 3 * BLOCK] + after
        into[:, 3 * BLOCK :] = scores[:, 3 * BLOCK :]

    def soften(source, into):
        for row in range(0, BLOCK, ROW_TILE):
            rows = slice(row, row + ROW_TILE)
            scores = source[rows, :]
            row_max = jnp.max(scores, axis=1, keepdims=True)
            weights = jnp.exp2((scores - row_max) * factor)
            total = jnp.sum(weights, axis=1, keepdims=True)
            into[rows, :] = (weights * (1.0 / total)).astype(jnp.bfloat16)

    def mix(at, source):
        _, places = listed(at)
        values = jnp.concatenate([value_all[p, s] for p, s in places], axis=0)
        mixed = jnp.dot(source[...], values, preferred_element_type=jnp.float32)
        out_ref[at] = mixed.astype(jnp.bfloat16)

    score(0, s_even)
    score(1, s_odd)
    soften(s_even, p_even)

    def two_blocks(step, carry):
        at = 2 * step
        score(at + 2, s_even)
        soften(s_odd, p_odd)
        mix(at, p_even)
        score(at + 3, s_odd)
        soften(s_even, p_even)
        mix(at + 1, p_odd)
        return carry

    lax.fori_loop(0, per_member // 2 - 1, two_blocks, 0, unroll=UNROLL)
    soften(s_odd, p_odd)
    mix(per_member - 2, p_even)
    mix(per_member - 1, p_odd)
    cots = jnp.concatenate([query_ref[at, BLOCK:, :] for at in range(per_member)], axis=1)
    grad_ref[...] = jnp.dot(
        cots,
        out_ref[...].reshape(per_member * BLOCK, HEAD_SIZE),
        preferred_element_type=jnp.float32,
    )

    lane = lax.broadcasted_iota(jnp.int32, (SUBLANES, LANES), 1) // shard

    def packed(source_ref, first):
        piece = jnp.zeros((SUBLANES, LANES), jnp.float32)
        for j in range(per_row):
            rows = source_ref[j * part_rows : j * part_rows + SUBLANES, :]
            turn = (j * shard - first) % LANES
            rows = pltpu.roll(rows, turn, 1) if turn else rows
            piece = jnp.where(lane == j, rows, piece)
        return piece

    own = packed(hold_ref, 0)
    for other in range(MEMBERS):
        piece = -LEARN_RATE * packed(grad_ref, other * shard)
        piece = piece + jnp.where(other == member, own, 0.0)
        for place in range(sent_ref.shape[0] // MEMBERS):
            sent_ref[place * MEMBERS + other] = piece


def stepped_of(got_ref, place):
    rows = [got_ref[place * MEMBERS + m] for m in range(MEMBERS)]
    return functools.reduce(jnp.add, rows)


def own_step(got_ref, out_ref):
    out_ref[...] = stepped_of(got_ref, lax.axis_index("upper"))


def blend(joints, hyper_ref, got_ref, own_ref, *refs):
    lower_refs, out_ref = refs[:-1], refs[-1]
    upper = lax.axis_index("upper")
    upper_bits = (got_ref.shape[0] // MEMBERS).bit_length() - 1
    shard = out_ref.shape[2]
    per_row = LANES // shard
    part_rows = joints // per_row
    lane = lax.broadcasted_iota(jnp.int32, (SUBLANES, LANES), 1) // shard
    row = lax.broadcasted_iota(jnp.int32, (SUBLANES, LANES), 0)
    joint = jnp.where(row < part_rows, lane * part_rows + row, joints)
    dims = jnp.zeros((SUBLANES, LANES), jnp.int32)
    for j in range(joints):
        dims = jnp.where(joint == j, hyper_ref[j], dims)
    own = own_ref[...]
    partner = own
    for bit, ref in enumerate(lower_refs):
        partner = jnp.where(dims == bit, ref[...], partner)
    for bit in range(upper_bits):
        other = stepped_of(got_ref, upper ^ (1 << bit))
        partner = jnp.where(dims == len(lower_refs) + bit, other, partner)
    mixed = 0.5 * (own + partner)
    for j in range(per_row):
        turn = (-j * shard) % LANES
        part = pltpu.roll(mixed, turn, 1) if turn else mixed
        for r in range(part_rows):
            out_ref[j * part_rows + r] = part[r : r + 1, :shard]


def local(queries, key_rows, value_rows, cotangent, readout, rand_blocks, global_blocks, hyper_dim):
    heads = lax.axis_size("head")
    uppers = lax.axis_size("upper")
    lowers = lax.axis_size("lower")
    joints = cotangent.shape[1]
    shard = readout.shape[2]
    listed = 3 + rand_blocks.shape[1] + global_blocks.shape[0]
    cot_rows = -(-joints // 32) * 32
    vmem = pl.BlockSpec(memory_space=pltpu.VMEM)
    smem = pl.BlockSpec(memory_space=pltpu.SMEM)
    away_spec = pl.BlockSpec(memory_space=pltpu.HBM)
    params = pltpu.CompilerParams(vmem_limit_bytes=VMEM_LIMIT)
    by_head = (heads, BLOCK, HEAD_SIZE)

    def near(value):
        return pltpu.with_memory_space_constraint(value, pltpu.VMEM)

    def away(value):
        return pltpu.with_memory_space_constraint(value, pltpu.HBM)

    def spread(value):
        return lax.all_to_all(value, "head", split_axis=0, concat_axis=0, tiled=True)

    def swap(value, distance):
        return lax.ppermute(value, "member", [(i, i ^ distance) for i in range(MEMBERS)])

    def split(rows):
        return pl.pallas_call(
            split_heads,
            out_shape=jax.ShapeDtypeStruct(by_head, rows.dtype),
            in_specs=[vmem],
            out_specs=vmem,
            compiler_params=params,
        )(rows)

    split_k = split(key_rows[0])
    k0 = spread(split_k)
    split_v = split(value_rows[0])
    v0 = spread(split_v)
    packed = pl.pallas_call(
        split_queries,
        out_shape=jax.ShapeDtypeStruct((heads, BLOCK + cot_rows, HEAD_SIZE), queries.dtype),
        in_specs=[vmem, vmem],
        out_specs=vmem,
        compiler_params=params,
        name="split_queries",
    )(queries[0], cotangent[0])
    q0 = spread(packed)
    k2 = swap(k0, 2)
    k1 = swap(k0, 1)
    k3 = swap(k2, 1)
    v2 = swap(v0, 2)
    v1 = swap(v0, 1)
    v3 = swap(v2, 1)
    mixed, sent = pl.pallas_call(
        functools.partial(attend, joints),
        out_shape=(
            jax.ShapeDtypeStruct(by_head, jnp.bfloat16),
            jax.ShapeDtypeStruct((uppers * MEMBERS, SUBLANES, LANES), jnp.float32),
        ),
        in_specs=[smem, smem, vmem] + [away_spec] * 3 + [vmem, away_spec] + [vmem] * 4,
        out_specs=(vmem, vmem),
        scratch_shapes=[
            pltpu.VMEM((MEMBERS, *by_head), jnp.bfloat16),
            pltpu.VMEM((MEMBERS, *by_head), jnp.bfloat16),
            pltpu.VMEM((cot_rows, HEAD_SIZE), jnp.float32),
            pltpu.VMEM((cot_rows, LANES), jnp.float32),
            pltpu.VMEM((BLOCK, listed * BLOCK), jnp.float32),
            pltpu.VMEM((BLOCK, listed * BLOCK), jnp.float32),
            pltpu.VMEM((BLOCK, listed * BLOCK), jnp.bfloat16),
            pltpu.VMEM((BLOCK, listed * BLOCK), jnp.bfloat16),
            pltpu.SemaphoreType.DMA((MEMBERS,)),
        ],
        compiler_params=params,
        name="attend",
    )(
        rand_blocks.T,
        global_blocks,
        near(q0),
        away(k0), away(k1), away(k2), near(k3),
        away(v0), near(v1), near(v2), near(v3),
        readout.reshape(joints, 1, shard),
    )
    got = lax.all_to_all(
        sent, ("upper", "member"), split_axis=0, concat_axis=0, tiled=True
    )
    returned = spread(mixed)
    piece = jax.ShapeDtypeStruct((SUBLANES, LANES), jnp.float32)
    stepped = pl.pallas_call(
        own_step,
        out_shape=piece,
        in_specs=[vmem],
        out_specs=vmem,
        compiler_params=params,
        name="own_step",
    )(near(got))
    partners = []
    for bit in range(lowers.bit_length() - 1):
        partners.append(lax.ppermute(stepped, "lower", [(i, i ^ 1 << bit) for i in range(lowers)]))
    attention = pl.pallas_call(
        join_heads,
        out_shape=jax.ShapeDtypeStruct((BLOCK, heads * HEAD_SIZE), returned.dtype),
        in_specs=[vmem],
        out_specs=vmem,
        compiler_params=params,
        name="join_heads",
    )(near(returned))
    new_readout = pl.pallas_call(
        functools.partial(blend, joints),
        out_shape=jax.ShapeDtypeStruct((joints, 1, shard), jnp.float32),
        in_specs=[smem] + [vmem] * (2 + len(partners)),
        out_specs=vmem,
        compiler_params=params,
        name="blend",
    )(hyper_dim, near(got), near(stepped), *map(near, partners))
    return (attention[None], new_readout.reshape(1, joints, shard))


def solution(mesh):
    replicas, group = mesh.devices.shape
    lowers = 1 << (replicas.bit_length() - 1) // 2
    fine = Mesh(
        mesh.devices.reshape(replicas // lowers, lowers, group // MEMBERS, MEMBERS),
        ("upper", "lower", "head", "member"),
    )
    rows = P(("upper", "lower"), ("head", "member"), None)
    columns = P(("upper", "lower"), None, ("head", "member"))
    return jax.shard_map(
        local,
        mesh=fine,
        in_specs=(rows, rows, rows, columns, columns, P(), P(), P()),
        out_specs=(rows, columns),
        check_vma=False,
    )
```

```python
import functools

import jax
import jax.numpy as jnp
from jax import lax
from jax.experimental import pallas as pl
from jax.experimental.pallas import tpu as pltpu
from jax.sharding import Mesh, PartitionSpec as P

BLOCK = 128
HEAD_SIZE = 128
LEARN_RATE = 0.01
MEMBERS = 4
MEMBER_BITS = 2
LANES = 128
VMEM_LIMIT = 20 << 20
UNROLL = True
ROW_TILE = 32
SUBLANES = 8
LOG2_E = 1.4426950408889634


def split_heads(rows_ref, out_ref):
    for head in range(out_ref.shape[0]):
        out_ref[head] = rows_ref[:, head * HEAD_SIZE : (head + 1) * HEAD_SIZE]


def split_queries(query_ref, cot_ref, out_ref):
    heads, rows, _ = out_ref.shape
    joints = cot_ref.shape[0]
    tail = jnp.concatenate(
        [cot_ref[...], jnp.zeros((rows - BLOCK - joints, BLOCK), cot_ref.dtype)], axis=0
    )
    for head in range(heads):
        out_ref[head, :BLOCK, :] = query_ref[:, head * HEAD_SIZE : (head + 1) * HEAD_SIZE]
        out_ref[head, BLOCK:, :] = tail


def join_heads(parts_ref, out_ref):
    for head in range(parts_ref.shape[0]):
        out_ref[:, head * HEAD_SIZE : (head + 1) * HEAD_SIZE] = parts_ref[head]


def attend(
    joints,
    listing_ref,
    query_ref,
    k0, k1, k2, k3,
    v0, v1, v2, v3,
    readout_ref,
    out_ref,
    sent_ref,
    key_all,
    value_all,
    grad_ref,
    hold_ref,
    s_even,
    s_odd,
    p_even,
    p_odd,
    sems,
):
    member = lax.axis_index("member")
    per_member = query_ref.shape[0]
    blocks = per_member * MEMBERS
    shard = readout_ref.shape[2]
    per_row = LANES // shard
    part_rows = joints // per_row
    early = ((k0, key_all.at[0]), (k1, key_all.at[1]), (k2, key_all.at[2]), (v0, value_all.at[0]))
    copies = [pltpu.make_async_copy(*pair, sems.at[at]) for at, pair in enumerate(early)]
    for copy in copies:
        copy.start()
    key_all[3] = k3[...]
    for at, source in ((1, v1), (2, v2), (3, v3)):
        value_all[at] = source[...]
    hold_ref[...] = jnp.zeros_like(hold_ref)
    for joint in range(joints):
        hold_ref[joint : joint + 1, :shard] = readout_ref[joint]
    for copy in copies:
        copy.wait()
    factor = (HEAD_SIZE ** (-0.5)) * LOG2_E

    def listed(at):
        block = at * MEMBERS + member
        ids = [block, jnp.maximum(block - 1, 0), jnp.minimum(block + 1, blocks - 1)]
        ids += [listing_ref[c, block] for c in range(listing_ref.shape[0])]
        return block, [((b & (MEMBERS - 1)) ^ member, b >> MEMBER_BITS) for b in ids]

    def score(at, into):
        block, places = listed(at)
        keys = jnp.concatenate([key_all[p, s] for p, s in places], axis=0)
        scores = lax.dot_general(
            query_ref[at, :BLOCK, :],
            keys,
            (((1,), (1,)), ((), ())),
            preferred_element_type=jnp.float32,
        )
        before = jnp.where(block >= 1, 0.0, -jnp.inf).astype(jnp.float32)
        after = jnp.where(block + 1 < blocks, 0.0, -jnp.inf).astype(jnp.float32)
        into[:, :BLOCK] = scores[:, :BLOCK]
        into[:, BLOCK : 2 * BLOCK] = scores[:, BLOCK : 2 * BLOCK] + before
        into[:, 2 * BLOCK : 3 * BLOCK] = scores[:, 2 * BLOCK : 3 * BLOCK] + after
        into[:, 3 * BLOCK :] = scores[:, 3 * BLOCK :]

    def soften(source, into):
        for row in range(0, BLOCK, ROW_TILE):
            rows = slice(row, row + ROW_TILE)
            scores = source[rows, :]
            row_max = jnp.max(scores, axis=1, keepdims=True)
            weights = jnp.exp2((scores - row_max) * factor)
            total = jnp.sum(weights, axis=1, keepdims=True)
            into[rows, :] = (weights * (1.0 / total)).astype(jnp.bfloat16)

    def mix(at, source):
        _, places = listed(at)
        values = jnp.concatenate([value_all[p, s] for p, s in places], axis=0)
        mixed = jnp.dot(source[...], values, preferred_element_type=jnp.float32)
        out_ref[at] = mixed.astype(jnp.bfloat16)

    score(0, s_even)
    score(1, s_odd)
    soften(s_even, p_even)

    def two_blocks(step, carry):
        at = 2 * step
        score(at + 2, s_even)
        soften(s_odd, p_odd)
        mix(at, p_even)
        score(at + 3, s_odd)
        soften(s_even, p_even)
        mix(at + 1, p_odd)
        return carry

    lax.fori_loop(0, per_member // 2 - 1, two_blocks, 0, unroll=UNROLL)
    soften(s_odd, p_odd)
    mix(per_member - 2, p_even)
    mix(per_member - 1, p_odd)
    cots = jnp.concatenate([query_ref[at, BLOCK:, :] for at in range(per_member)], axis=1)
    grad_ref[...] = jnp.dot(
        cots,
        out_ref[...].reshape(per_member * BLOCK, HEAD_SIZE),
        preferred_element_type=jnp.float32,
    )

    lane = lax.broadcasted_iota(jnp.int32, (SUBLANES, LANES), 1) // shard

    def packed(source_ref, first):
        piece = jnp.zeros((SUBLANES, LANES), jnp.float32)
        for j in range(per_row):
            rows = source_ref[j * part_rows : j * part_rows + SUBLANES, :]
            turn = (j * shard - first) % LANES
            rows = pltpu.roll(rows, turn, 1) if turn else rows
            piece = jnp.where(lane == j, rows, piece)
        return piece

    own = packed(hold_ref, 0)
    for other in range(MEMBERS):
        piece = -LEARN_RATE * packed(grad_ref, other * shard)
        piece = piece + jnp.where(other == member, own, 0.0)
        for place in range(sent_ref.shape[0] // MEMBERS):
            sent_ref[place * MEMBERS + other] = piece


def stepped_of(got_ref, place):
    rows = [got_ref[place * MEMBERS + m] for m in range(MEMBERS)]
    return functools.reduce(jnp.add, rows)


def own_step(got_ref, out_ref):
    out_ref[...] = stepped_of(got_ref, lax.axis_index("upper"))


def blend(joints, hyper_ref, got_ref, own_ref, *refs):
    lower_refs, out_ref = refs[:-1], refs[-1]
    upper = lax.axis_index("upper")
    upper_bits = (got_ref.shape[0] // MEMBERS).bit_length() - 1
    shard = out_ref.shape[2]
    per_row = LANES // shard
    part_rows = joints // per_row
    lane = lax.broadcasted_iota(jnp.int32, (SUBLANES, LANES), 1) // shard
    row = lax.broadcasted_iota(jnp.int32, (SUBLANES, LANES), 0)
    joint = jnp.where(row < part_rows, lane * part_rows + row, joints)
    dims = jnp.zeros((SUBLANES, LANES), jnp.int32)
    for j in range(joints):
        dims = jnp.where(joint == j, hyper_ref[j], dims)
    own = own_ref[...]
    partner = own
    lower = lax.axis_index("lower")
    lower_bits = len(lower_refs) // 2
    for bit in range(lower_bits):
        below, above = lower_refs[bit][...], lower_refs[lower_bits + bit][...]
        if bit == 0:
            above = jnp.where(lower == 1, above, lower_refs[-1][...])
        got = jnp.where((lower >> bit) & 1 == 0, below, above)
        partner = jnp.where(dims == bit, got, partner)
    for bit in range(upper_bits):
        other = stepped_of(got_ref, upper ^ (1 << bit))
        partner = jnp.where(dims == lower_bits + bit, other, partner)
    mixed = 0.5 * (own + partner)
    for j in range(per_row):
        turn = (-j * shard) % LANES
        part = pltpu.roll(mixed, turn, 1) if turn else mixed
        for r in range(part_rows):
            out_ref[j * part_rows + r] = part[r : r + 1, :shard]


def local(queries, key_rows, value_rows, cotangent, readout, rand_blocks, global_blocks, hyper_dim):
    heads = lax.axis_size("head")
    uppers = lax.axis_size("upper")
    lowers = lax.axis_size("lower")
    joints = cotangent.shape[1]
    shard = readout.shape[2]
    listed = 3 + rand_blocks.shape[1] + global_blocks.shape[0]
    cot_rows = -(-joints // SUBLANES) * SUBLANES
    vmem = pl.BlockSpec(memory_space=pltpu.VMEM)
    smem = pl.BlockSpec(memory_space=pltpu.SMEM)
    away_spec = pl.BlockSpec(memory_space=pltpu.HBM)
    params = pltpu.CompilerParams(vmem_limit_bytes=VMEM_LIMIT)
    by_head = (heads, BLOCK, HEAD_SIZE)

    def near(value):
        return pltpu.with_memory_space_constraint(value, pltpu.VMEM)

    def away(value):
        return pltpu.with_memory_space_constraint(value, pltpu.HBM)

    def spread(value):
        return lax.all_to_all(value, "head", split_axis=0, concat_axis=0, tiled=True)

    def swap(value, distance):
        return lax.ppermute(value, "member", [(i, i ^ distance) for i in range(MEMBERS)])

    def split(rows):
        return pl.pallas_call(
            split_heads,
            out_shape=jax.ShapeDtypeStruct(by_head, rows.dtype),
            in_specs=[vmem],
            out_specs=vmem,
            compiler_params=params,
        )(rows)

    listing = jnp.concatenate(
        [rand_blocks.T, jnp.broadcast_to(global_blocks[:, None], (global_blocks.shape[0], rand_blocks.shape[0]))]
    )
    split_k = split(key_rows[0])
    k0 = spread(split_k)
    split_v = split(value_rows[0])
    v0 = spread(split_v)
    packed = pl.pallas_call(
        split_queries,
        out_shape=jax.ShapeDtypeStruct((heads, BLOCK + cot_rows, HEAD_SIZE), queries.dtype),
        in_specs=[vmem, vmem],
        out_specs=vmem,
        compiler_params=params,
        name="split_queries",
    )(queries[0], cotangent[0])
    q0 = spread(packed)
    k2 = swap(k0, 2)
    k1 = swap(k0, 1)
    k3 = swap(k2, 1)
    v2 = swap(v0, 2)
    v1 = swap(v0, 1)
    v3 = swap(v2, 1)
    mixed, sent = pl.pallas_call(
        functools.partial(attend, joints),
        out_shape=(
            jax.ShapeDtypeStruct(by_head, jnp.bfloat16),
            jax.ShapeDtypeStruct((uppers * MEMBERS, SUBLANES, LANES), jnp.float32),
        ),
        in_specs=[smem, vmem] + [away_spec] * 3 + [vmem, away_spec] + [vmem] * 4,
        out_specs=(vmem, vmem),
        scratch_shapes=[
            pltpu.VMEM((MEMBERS, *by_head), jnp.bfloat16),
            pltpu.VMEM((MEMBERS, *by_head), jnp.bfloat16),
            pltpu.VMEM((cot_rows, HEAD_SIZE), jnp.float32),
            pltpu.VMEM((cot_rows, LANES), jnp.float32),
            pltpu.VMEM((BLOCK, listed * BLOCK), jnp.float32),
            pltpu.VMEM((BLOCK, listed * BLOCK), jnp.float32),
            pltpu.VMEM((BLOCK, listed * BLOCK), jnp.bfloat16),
            pltpu.VMEM((BLOCK, listed * BLOCK), jnp.bfloat16),
            pltpu.SemaphoreType.DMA((MEMBERS,)),
        ],
        compiler_params=params,
        name="attend",
    )(
        listing,
        near(q0),
        away(k0), away(k1), away(k2), near(k3),
        away(v0), near(v1), near(v2), near(v3),
        readout.reshape(joints, 1, shard),
    )
    got = lax.all_to_all(
        sent, ("upper", "member"), split_axis=0, concat_axis=0, tiled=True
    )
    returned = spread(mixed)
    piece = jax.ShapeDtypeStruct((SUBLANES, LANES), jnp.float32)
    stepped = pl.pallas_call(
        own_step,
        out_shape=piece,
        in_specs=[vmem],
        out_specs=vmem,
        compiler_params=params,
        name="own_step",
    )(near(got))

    def passed(bit, senders):
        pairs = [(i, i ^ 1 << bit) for i in senders]
        return lax.ppermute(stepped, "lower", pairs) if pairs else stepped

    bits = range(lowers.bit_length() - 1)
    ones = [[i for i in range(lowers) if i >> bit & 1] for bit in bits]
    zeros = [[i for i in range(lowers) if not i >> bit & 1] for bit in bits]
    partners = [passed(bit, ones[bit]) for bit in bits]
    if partners:
        partners.append(passed(0, zeros[0][:1]))
        partners += [passed(bit, zeros[bit]) for bit in bits[1:]]
        partners.append(passed(0, zeros[0][1:]))
    attention = pl.pallas_call(
        join_heads,
        out_shape=jax.ShapeDtypeStruct((BLOCK, heads * HEAD_SIZE), returned.dtype),
        in_specs=[vmem],
        out_specs=vmem,
        compiler_params=params,
        name="join_heads",
    )(near(returned))
    new_readout = pl.pallas_call(
        functools.partial(blend, joints),
        out_shape=jax.ShapeDtypeStruct((joints, 1, shard), jnp.float32),
        in_specs=[smem] + [vmem] * (2 + len(partners)),
        out_specs=vmem,
        compiler_params=params,
        name="blend",
    )(hyper_dim, near(got), near(stepped), *map(near, partners))
    return (attention[None], new_readout.reshape(1, joints, shard))


def solution(mesh):
    replicas, group = mesh.devices.shape
    lowers = 1 << (replicas.bit_length() - 1) // 2
    fine = Mesh(
        mesh.devices.reshape(replicas // lowers, lowers, group // MEMBERS, MEMBERS),
        ("upper", "lower", "head", "member"),
    )
    rows = P(("upper", "lower"), ("head", "member"), None)
    columns = P(("upper", "lower"), None, ("head", "member"))
    return jax.shard_map(
        local,
        mesh=fine,
        in_specs=(rows, rows, rows, columns, columns, P(), P(), P()),
        out_specs=(rows, columns),
        check_vma=False,
    )
```
